128 devices in a mesh: req: 16 (over x, y_lo, core), head: 8 (over z, y_hi).
Axes of the slice: x: 4, y: 4 (y_hi: 2, y_lo: 2; y = y_hi * 2 + y_lo), z: 4, core: 2. Of those that a mesh axis runs over, the one named last changes fastest.
Arguments:
- tokens: bfloat16 [32768, 2048], P(('req', 'head')), may hold values from -6 to 6
- input_gain: float32 [2048], replicated, may hold values from 0.1 to 1.9
- w_query: bfloat16 [2048, 2048], replicated, may hold values from -0.125 to 0.125
- w_keyval: bfloat16 [2048, 1024], replicated, may hold values from -0.125 to 0.125
- query_gain: float32 [256], replicated, may hold values from 0.1 to 1.9
- key_gain: float32 [256], replicated, may hold values from 0.1 to 1.9
- w_output: bfloat16 [2048, 2048], P('req'), may hold values from -0.125 to 0.125
- laurel_left: bfloat16 [2048, 64], replicated, may hold values from -0.125 to 0.125
- laurel_right: bfloat16 [64, 2048], replicated, may hold values from -0.75 to 0.75
- laurel_gain: float32 [2048], replicated, may hold values from 0.1 to 1.9
- post_gain: float32 [2048], replicated, may hold values from 0.1 to 1.9
- cache_pool: bfloat16 [1024, 64, 1024], P('req'), may hold values from -200 to 200, as said below
- page_table: int32 [64, 16], replicated, may hold values from 0 to 63, as said below
- cached_len: int32 [64], replicated, may hold values from 0 to 1024, as said below
- slot_of: int32 [64], replicated, may hold values from 0 to 63, as said below
Outputs:
- mixed: bfloat16 [32768, 2048], P(('req', 'head'))
The draws below stay inside these ranges and needn't reach their ends.
Inputs may be any that keep to these rules, and one draw needn't show every extreme that they name: slot_of is a permutation of the 64 requests onto slots. Request i's pages lie in group i // 4. In each group exactly one request is served by the group before it and exactly one by the group after it (group indices cyclic over 16); all others are served by their own group. `page_table`: page p of request i holds its cached positions p*64 to (p+1)*64 - 1; the rows of the 4 requests of one group together name each of that group's 64 pages once. `cached_len`: at least one request that changes group has exactly 1024 cached positions, and some request has none. `cache_pool`: stored keys (already normalized and rotated) and values; entries past a request's cached length are arbitrary.
All inputs are finite; a program needn't handle non-finite values.
Results may differ from the reference program's by a relative error of at most 0.012.
The reference program's roundings to bfloat16 on the way (of `normed`, `query`, `key`, `value`, `weights`, `attended` and `low`) count: a program that leaves them out, or rounds other values in their place, can miss the bound.
Values may be sent and summed in bfloat16 or wider, within the bound.
A program may use at most 128 MiB of HBM per device.

```python
import math
import jax
import jax.numpy as jnp
from jax import lax

D = 2048
NH = 8
KVH = 2
HD = 256
RANK = 64
REQ_DEV = 4
CH = 512
LMAX = 1024
PAGE = 64
MAXP = 16
POOL = 64
GROUPS = 16
NREQ = 64
NTOK = 32768


def mover_order(key):
    groups = NREQ // REQ_DEV
    subkeys = jax.random.split(jax.random.fold_in(key, 7), groups)
    return jax.vmap(lambda subkey: jax.random.permutation(subkey, REQ_DEV))(subkeys).astype(jnp.int32)


def draw_slot_of(key, part):
    groups = NREQ // REQ_DEV
    order = mover_order(key)
    group_ids = jnp.arange(groups, dtype=jnp.int32)
    staying = group_ids[:, None] * REQ_DEV + order[:, 2:]
    from_after = ((group_ids + 1) % groups * REQ_DEV + jnp.roll(order[:, 0], -1))[:, None]
    from_before = ((group_ids + groups - 1) % groups * REQ_DEV + jnp.roll(order[:, 1], 1))[:, None]
    members = jnp.concatenate([staying, from_after, from_before], axis=1)
    subkeys = jax.random.split(jax.random.fold_in(key, 9), groups)
    shuffle = jax.vmap(lambda subkey: jax.random.permutation(subkey, REQ_DEV))(subkeys).astype(jnp.int32)
    placed = jnp.take_along_axis(members, shuffle, axis=1)
    return jnp.zeros((NREQ,), jnp.int32).at[placed.reshape(-1)].set(jnp.arange(NREQ, dtype=jnp.int32))


def draw_cached_len(key, part):
    groups = NREQ // REQ_DEV
    order = mover_order(key)
    lengths = jax.random.randint(jax.random.fold_in(key, 3), (NREQ,), LMAX // 2, LMAX + 1).astype(jnp.int32)
    chosen = jax.random.randint(jax.random.fold_in(key, 5), (), 0, groups)
    lengths = lengths.at[chosen * REQ_DEV + order[chosen, 0]].set(LMAX)
    other = (chosen + 1) % groups
    lengths = lengths.at[other * REQ_DEV + order[other, REQ_DEV - 1]].set(0)
    return lengths


def draw_page_table(key, part):
    groups = NREQ // REQ_DEV
    subkeys = jax.random.split(jax.random.fold_in(key, 13), groups)
    pages = jax.vmap(lambda subkey: jax.random.permutation(subkey, POOL))(subkeys)
    return pages.reshape(NREQ, MAXP).astype(jnp.int32)


def draw_cache_pool(key, part):
    rows = GROUPS * POOL
    values = jnp.clip(jax.random.normal(jax.random.fold_in(key, 24), (rows, PAGE, 2 * KVH, HD), jnp.float32), -6.0, 6.0)
    return values.reshape(rows, PAGE, 2 * KVH * HD).astype(jnp.bfloat16)


def level_of(rng, extent, shards, low, top_value):
    level = 1.0
    for axis_at, blocks in shards:
        steps = jax.random.uniform(jax.random.fold_in(jax.random.fold_in(rng, 6), axis_at), (blocks,), jnp.float32, low / len(shards), top_value / len(shards))
        level = level * jnp.repeat(jnp.exp(steps), extent[axis_at] // blocks).reshape((-1,) + (1,) * (len(extent) - 1 - axis_at))
    return level


def normal_values(stream_key, shape, width, most, pieces=(), kind=jnp.bfloat16):
    gain = level_of(stream_key, shape, pieces, -0.22, 0.18) if pieces else 1.0
    values = jax.random.normal(stream_key, shape, jnp.float32) * width * gain
    return jnp.minimum(jnp.maximum(values, -most), most).astype(kind)


def setup_inputs(seed: int = 0) -> dict:
    streams_of = jax.random.split(jax.random.key(seed), 16)
    return {
        "tokens": normal_values(streams_of[0], (NTOK, D), 1.0, 6.0, ((0, 128),)),
        "input_gain": jnp.clip(1.0 + 0.18 * jax.random.normal(streams_of[1], (D,), jnp.float32), 0.1, 1.9),
        "w_query": normal_values(streams_of[2], (D, NH * HD), D ** -0.5, 0.125),
        "w_keyval": normal_values(streams_of[3], (D, 2 * KVH * HD), D ** -0.5, 0.125),
        "query_gain": jnp.clip(1.0 + 0.18 * jax.random.normal(streams_of[4], (HD,), jnp.float32), 0.1, 1.9),
        "key_gain": jnp.clip(1.0 + 0.18 * jax.random.normal(streams_of[5], (HD,), jnp.float32), 0.1, 1.9),
        "w_output": normal_values(streams_of[6], (NH * HD, D), (NH * HD) ** -0.5, 0.125, ((0, 16),)),
        "laurel_left": normal_values(streams_of[7], (D, RANK), D ** -0.5, 0.125),
        "laurel_right": normal_values(streams_of[8], (RANK, D), RANK ** -0.5, 0.75),
        "laurel_gain": jnp.clip(1.0 + 0.18 * jax.random.normal(streams_of[9], (D,), jnp.float32), 0.1, 1.9),
        "post_gain": jnp.clip(1.0 + 0.18 * jax.random.normal(streams_of[10], (D,), jnp.float32), 0.1, 1.9),
        "cache_pool": draw_cache_pool(jax.random.fold_in(streams_of[15], 71), 0),
        "page_table": draw_page_table(jax.random.fold_in(streams_of[15], 71), 0),
        "cached_len": draw_cached_len(jax.random.fold_in(streams_of[15], 71), 0),
        "slot_of": draw_slot_of(jax.random.fold_in(streams_of[15], 71), 0),
    }


epsilon = 1e-06

def normalize(values_in):
    return values_in * lax.rsqrt(lax.optimization_barrier(jnp.mean(values_in * values_in, axis=-1, keepdims=True)) + epsilon)

def rotate(values_in, position):
    half = values_in.shape[-1] // 2
    exponent = jnp.arange(half, dtype=jnp.float32) * (2.0 / values_in.shape[-1])
    inverse = jnp.power(jnp.float32(1000000.0), -exponent)
    angle = position.astype(jnp.float32)[:, None] * inverse[None, :]
    cosine = jnp.cos(angle)[:, None, :]
    sine = jnp.sin(angle)[:, None, :]
    first_half = values_in[..., :half]
    second_half = values_in[..., half:]
    return jnp.concatenate([first_half * cosine - second_half * sine, second_half * cosine + first_half * sine], axis=-1)

def reference(tokens, input_gain, w_query, w_keyval, query_gain, key_gain, w_output, laurel_left, laurel_right, laurel_gain, post_gain, cache_pool, page_table, cached_len, slot_of):
    inputs = tokens.astype(jnp.float32)
    normed = (normalize(inputs) * input_gain).astype(jnp.bfloat16)
    query_raw = jnp.dot(normed, w_query, preferred_element_type=jnp.float32)
    keyval_raw = jnp.dot(normed, w_keyval, preferred_element_type=jnp.float32)
    slots = jnp.arange(NREQ, dtype=jnp.int32)
    matches = slot_of[None, :] == slots[:, None]
    request_at = lax.optimization_barrier(jnp.sum(jnp.where(matches, slots[None, :], 0), axis=1)).astype(jnp.int32)
    starts = jnp.take(cached_len, request_at)
    position = jnp.repeat(starts, CH) + jnp.tile(jnp.arange(CH, dtype=jnp.int32), NREQ)
    query = rotate(normalize(query_raw.reshape(NTOK, NH, HD)) * query_gain, position).astype(jnp.bfloat16)
    keyval = keyval_raw.reshape(NTOK, KVH, 2, HD)
    key = rotate(normalize(keyval[:, :, 0]) * key_gain, position).astype(jnp.bfloat16)
    value = normalize(keyval[:, :, 1]).astype(jnp.bfloat16)
    per_group = NH // KVH
    score_scale = HD ** (-0.5)
    cached_rows = MAXP * PAGE

    def one_slot(slot):
        request = jnp.take(request_at, slot)
        home_group = request // REQ_DEV
        length = jnp.take(cached_len, request)
        pages = home_group * POOL + jnp.take(page_table, request, axis=0)
        stored = jnp.take(cache_pool, pages, axis=0).reshape(cached_rows, KVH, 2, HD)
        begin = (slot * CH).astype(jnp.int32)
        block_queries = lax.dynamic_slice_in_dim(query, begin, CH, 0).astype(jnp.float32)
        fresh_keys = lax.dynamic_slice_in_dim(key, begin, CH, 0)
        fresh_values = lax.dynamic_slice_in_dim(value, begin, CH, 0)
        all_keys = jnp.repeat(jnp.concatenate([stored[:, :, 0], fresh_keys], axis=0), per_group, axis=1)
        all_values = jnp.repeat(jnp.concatenate([stored[:, :, 1], fresh_values], axis=0), per_group, axis=1)
        scores = jnp.einsum('tnh,knh->ntk', block_queries, all_keys.astype(jnp.float32)) * score_scale
        cached_seen = jnp.broadcast_to((jnp.arange(cached_rows) < length)[None, :], (CH, cached_rows))
        causal = jnp.arange(CH)[None, :] <= jnp.arange(CH)[:, None]
        visible = jnp.concatenate([cached_seen, causal], axis=1)[None]
        highest = lax.optimization_barrier(jnp.max(jnp.where(visible, scores, -jnp.inf), axis=-1, keepdims=True))
        expd = jnp.where(visible, jnp.exp(scores - highest), 0.0)
        weights = (expd / lax.optimization_barrier(jnp.sum(expd, axis=-1, keepdims=True))).astype(jnp.bfloat16)
        result = jnp.einsum('ntk,knh->tnh', weights.astype(jnp.float32), all_values.astype(jnp.float32))
        return result.astype(jnp.bfloat16).reshape(CH, NH * HD)
    attended = lax.map(one_slot, slots).reshape(NTOK, NH * HD)
    projected = jnp.dot(attended, w_output, preferred_element_type=jnp.float32)
    attn = normalize(projected) * post_gain
    low = jnp.dot(normed, laurel_left, preferred_element_type=jnp.float32).astype(jnp.bfloat16)
    laurel = normed.astype(jnp.float32) + normalize(jnp.dot(low, laurel_right, preferred_element_type=jnp.float32)) * laurel_gain
    return ((attn + inputs + laurel) / math.sqrt(2.0)).astype(jnp.bfloat16)
```

```python
import functools
import math

import jax
import jax.numpy as jnp
from jax import lax
from jax.experimental import pallas as pl
from jax.experimental.pallas import tpu as pltpu
from jax.sharding import PartitionSpec as P

MESH = pl.DeviceIdType.MESH
F32 = jnp.float32
BF16 = jnp.bfloat16

D = 2048
NH = 8
KVH = 2
HD = 256
HALF = HD // 2
RANK = 64
REQ_DEV = 4
CH = 512
LMAX = 1024
PAGE = 64
MAXP = 16
GROUPS = 16
NREQ = 64
ROWS = 256
KVW = 2 * KVH * HD
WROWS = D // GROUPS
UNIT = WROWS // 4
QPAGES = MAXP // 4
HPAGES = QPAGES // 2
EPS = 1e-06
VMEM_LIMIT = 64 * 1024 * 1024 - 128 * 1024


def place():
    group = lax.axis_index("req")
    member = lax.axis_index("head")
    x = group // 4
    y_lo = (group // 2) % 2
    core = group % 2
    z = member // 2
    y_hi = member % 2
    return group, x, y_lo, core, z, y_hi


def gather_kernel(table, slots, pool, own, chip, cross, sems):
    group, _, _, core, z, y_hi = place()
    slot = group * REQ_DEV + z
    request = lax.fori_loop(
        0, NREQ, lambda i, found: jnp.where(slots[i] == slot, i, found), jnp.int32(0)
    )
    partner = group + 1 - 2 * core
    across = (group + 2 * core - 1 + GROUPS) % GROUPS
    base = group * REQ_DEV
    to_chip = base
    to_cross = base
    for i in range(REQ_DEV):
        aim = slots[base + i] // REQ_DEV
        to_chip = jnp.where(aim == partner, base + i, to_chip)
        to_cross = jnp.where(aim == across, base + i, to_cross)
    copies = []
    first = z * QPAGES + y_hi * HPAGES
    for p in range(HPAGES):
        copies.append((table[to_cross * MAXP + first + p], cross.at[pl.ds(p * PAGE, PAGE)]))
    for p in range(MAXP):
        copies.append((table[to_chip * MAXP + p], chip.at[pl.ds(p * PAGE, PAGE)]))
    for p in range(MAXP):
        copies.append((table[request * MAXP + p], own.at[pl.ds(p * PAGE, PAGE)]))
    started = [
        pltpu.make_async_copy(pool.at[page], target, sems.at[i])
        for i, (page, target) in enumerate(copies)
    ]
    for copy in started:
        copy.start()
    for copy in started:
        copy.wait()


def gather_pages(page_table, slot_of, cache_pool):
    smem = pl.BlockSpec(memory_space=pltpu.SMEM)
    vmem = pl.BlockSpec(memory_space=pltpu.VMEM)
    return pl.pallas_call(
        gather_kernel,
        out_shape=(
            jax.ShapeDtypeStruct((LMAX, KVW), BF16),
            jax.ShapeDtypeStruct((LMAX, KVW), BF16),
            jax.ShapeDtypeStruct((HPAGES * PAGE, KVW), BF16),
        ),
        in_specs=[smem, smem, pl.BlockSpec(memory_space=pl.ANY)],
        out_specs=(vmem, vmem, vmem),
        scratch_shapes=[pltpu.SemaphoreType.DMA((2 * MAXP + HPAGES,))],
        name="gather_pages",
    )(page_table.reshape(-1), slot_of, cache_pool)


N_COPIES = 64
CROSS_ID = 1


def params(**kw):
    return pltpu.CompilerParams(vmem_limit_bytes=VMEM_LIMIT, **kw)


def comm_kernel(w_ref, chip_ref, cross_ref, full, chip_in, cross_in, ssem, rsem, lsem):
    group, x, yl, c, z, h = place()

    def dev(ax, ayl, ac, az, ah):
        return (ax * 4 + ayl * 2 + ac, az * 2 + ah)

    xp, xm, x2 = (x + 1) % 4, (x + 3) % 4, (x + 2) % 4
    zp, zm, z2 = (z + 1) % 4, (z + 3) % 4, (z + 2) % 4
    ol = 1 - yl
    to_xp, to_xm = dev(xp, yl, c, z, h), dev(xm, yl, c, z, h)
    to_zp, to_zm = dev(x, yl, c, zp, h), dev(x, yl, c, zm, h)
    to_s, to_c = dev(x, ol, c, z, h), dev(x, ol, c, z, 1 - h)
    to_p = dev(x, yl, 1 - c, z, h)
    across = (group + 2 * c - 1 + GROUPS) % GROUPS
    to_t = [(across, z * 2 + h), (across, z * 2 + 1 - h)]

    barrier = pltpu.get_barrier_semaphore()
    others = [to_xp, to_xm, to_zp, to_zm, to_s, to_c, to_p] + to_t
    for other in others:
        pl.semaphore_signal(barrier, inc=1, device_id=other, device_id_type=MESH)
    pl.semaphore_wait(barrier, len(others))

    sent = []

    def send(src, dst, to):
        i = len(sent)
        copy = pltpu.make_async_remote_copy(
            src_ref=src,
            dst_ref=dst,
            send_sem=ssem.at[i],
            recv_sem=rsem.at[i],
            device_id=to,
            device_id_type=MESH,
        )
        copy.start()
        sent.append(copy)
        return copy

    def rows(ax, ayl, unit, n):
        start = (ax * 4 + ayl * 2 + c) * WROWS + unit * UNIT
        return full.at[pl.ds(pl.multiple_of(start, UNIT), n * UNIT)]

    def mine(unit, n):
        return w_ref.at[pl.ds(unit * UNIT, n * UNIT)]

    def pages(az, rel, p, n):
        half = h if rel == 0 else 1 - h
        start = (az * QPAGES + half * HPAGES + p) * PAGE
        return cross_in.at[pl.ds(pl.multiple_of(start, PAGE), n * PAGE)]

    def relay(ref, to):
        return send(ref, ref, to)

    own_copy = pltpu.make_async_copy(w_ref, rows(x, yl, 0, 4), lsem)
    own_copy.start()
    crossing = []
    for p in range(HPAGES):
        for rel in range(2):
            target = (z * QPAGES + h * HPAGES + p) * PAGE
            crossing.append(
                send(
                    cross_ref.at[pl.ds(p * PAGE, PAGE)],
                    cross_in.at[pl.ds(pl.multiple_of(target, PAGE), PAGE)],
                    to_t[rel],
                )
            )
    a1 = [send(mine(0, 2), rows(x, yl, 0, 2), to) for to in (to_xp, to_xm)]
    b1 = [send(mine(2, 1), rows(x, yl, 2, 1), to_s), send(mine(3, 1), rows(x, yl, 3, 1), to_c)]
    chip_copy = send(chip_ref, chip_in, to_p)
    last = [send(w_ref, rows(x, yl, 0, 4), to_p), chip_copy]
    b2 = [send(mine(2, 2), rows(x, yl, 2, 2), to) for to in (to_xp, to_xm)]
    last += [send(mine(0, 1), rows(x, yl, 0, 1), to_s), send(mine(1, 1), rows(x, yl, 1, 1), to_c)]

    ring = []
    for p in range(HPAGES):
        for rel in range(2):
            crossing[2 * p + rel].wait_recv()
            for to in (to_zp, to_zm):
                ring.append(relay(pages(z, rel, p, 1), to))
    for copy in b1:
        copy.wait_recv()
    b2y = [relay(rows(x, ol, 2, 2), to) for to in (to_xp, to_xm)]
    last.append(relay(rows(x, ol, 2, 2), to_p))
    for copy in a1:
        copy.wait_recv()
    a2 = [relay(rows(xm, yl, 0, 1), to_xp), relay(rows(xp, yl, 1, 1), to_xm)]
    for ax in (xm, xp):
        last += [relay(rows(ax, yl, 0, 1), to_s), relay(rows(ax, yl, 1, 1), to_c)]
        last.append(relay(rows(ax, yl, 0, 2), to_p))
    for copy in b2:
        copy.wait_recv()
    b3 = [relay(rows(xm, yl, 2, 1), to_xp), relay(rows(xp, yl, 3, 1), to_xm)]
    for ax in (xm, xp):
        last.append(relay(rows(ax, yl, 2, 2), to_p))
    for p in range(HPAGES):
        for rel in range(2):
            one, two = ring[4 * p + 2 * rel], ring[4 * p + 2 * rel + 1]
            one.wait_recv()
            two.wait_recv()
            last.append(relay(pages(zm, 0, p, 1), to_zp) if rel == 0 else relay(pages(zp, 1, p, 1), to_zm))
    for copy in a2:
        copy.wait_recv()
    last += [relay(rows(x2, yl, 0, 1), to_s), relay(rows(x2, yl, 1, 1), to_c)]
    last.append(relay(rows(x2, yl, 0, 2), to_p))
    for copy in b2y:
        copy.wait_recv()
    b3 += [relay(rows(xm, ol, 2, 1), to_xp), relay(rows(xp, ol, 3, 1), to_xm)]
    for ax in (xm, xp):
        last.append(relay(rows(ax, ol, 2, 2), to_p))
    for copy in b3:
        copy.wait_recv()
    last.append(relay(rows(x2, yl, 2, 2), to_p))
    last.append(relay(rows(x2, ol, 2, 2), to_p))
    yin = [last[i] for i in (2, 3, 5, 6, 8, 9)]
    yin += [last[i] for i in (17, 18)]
    for i, ax in enumerate((x, xm, xp, x2)):
        yin[2 * i].wait_recv()
        yin[2 * i + 1].wait_recv()
        last.append(relay(rows(ax, ol, 0, 2), to_p))
    own_copy.wait()
    for copy in last:
        if not any(copy is done for done in yin):
            copy.wait_recv()
    for copy in sent:
        copy.wait_send()


def exchange(w_output, chip, cross):
    vmem = pl.BlockSpec(memory_space=pltpu.VMEM)
    return pl.pallas_call(
        comm_kernel,
        out_shape=(
            jax.ShapeDtypeStruct((D, D), BF16),
            jax.ShapeDtypeStruct((LMAX, KVW), BF16),
            jax.ShapeDtypeStruct((LMAX, KVW), BF16),
        ),
        in_specs=[vmem, vmem, vmem],
        out_specs=(vmem, vmem, vmem),
        scratch_shapes=[
            pltpu.SemaphoreType.DMA((N_COPIES,)),
            pltpu.SemaphoreType.DMA((N_COPIES,)),
            pltpu.SemaphoreType.DMA,
        ],
        compiler_params=params(collective_id=0, has_side_effects=True),
        name="exchange",
    )(w_output, chip, cross)


def rms(values):
    return lax.rsqrt(jnp.mean(values * values, axis=-1, keepdims=True) + EPS)


def dot(a, b):
    return jnp.dot(a, b, preferred_element_type=F32)


def rotated(values, cosine, sine):
    a, b = values[:, :HALF], values[:, HALF:]
    return jnp.concatenate([a * cosine - b * sine, b * cosine + a * sine], axis=-1)


def project_kernel(
    tokens, in_gain, wq, wkv, q_gain, k_gain, left, right, l_gain, cosine, sine,
    query, kv, side, normed,
):
    inputs = tokens[...].astype(F32)
    normed[...] = (inputs * rms(inputs) * in_gain[...]).astype(BF16)
    cos, sin = cosine[...], sine[...]
    for g in range(KVH):
        raw = dot(normed[...], wkv[:, 2 * g * HD : (2 * g + 2) * HD])
        key, value = raw[:, :HD], raw[:, HD:]
        key = rotated(key * rms(key) * k_gain[...], cos, sin)
        kv[:, 2 * g * HD : (2 * g + 1) * HD] = key.astype(BF16)
        kv[:, (2 * g + 1) * HD : (2 * g + 2) * HD] = (value * rms(value)).astype(BF16)

    def head(n, carry):
        raw = dot(normed[...], wq[:, pl.ds(pl.multiple_of(n * HD, HD), HD)])
        raw = rotated(raw * rms(raw) * q_gain[...], cosine[...], sine[...])
        query[n] = raw.astype(BF16)
        return carry

    lax.fori_loop(0, NH, head, 0)
    low = dot(normed[...], left[...]).astype(BF16)
    u = dot(low, right[...])
    laurel = normed[...].astype(F32) + u * rms(u) * l_gain[...]
    side[...] = tokens[...].astype(F32) + laurel


def attend_kernel(
    lens, slots, query, kv, other, own, chip_in, cross_in, full, side, p_gain,
    mixed, store, attended, projected, sems,
):
    group, _, _, core, z, y_hi = place()
    slot = group * REQ_DEV + z
    request = lax.fori_loop(
        0, NREQ, lambda i, found: jnp.where(slots[i] == slot, i, found), jnp.int32(0)
    )
    length = lens[request]
    home = request // REQ_DEV
    partner = group + 1 - 2 * core
    for want, source in (
        (home == group, own),
        (home == partner, chip_in),
        ((home != group) & (home != partner), cross_in),
    ):

        @pl.when(want)
        def _():
            copy = pltpu.make_async_copy(source, store, sems.at[0])
            copy.start()
            copy.wait()

    def contract(a, b):
        return lax.dot_general(a, b, (((1,), (1,)), ((), ())), preferred_element_type=F32)

    seen = lax.broadcasted_iota(jnp.int32, (1, LMAX), 1) < length
    causal = lax.broadcasted_iota(jnp.int32, (ROWS, ROWS), 1) <= lax.broadcasted_iota(
        jnp.int32, (ROWS, ROWS), 0
    )
    for g in range(KVH):
        k0, v0, end = 2 * g * HD, (2 * g + 1) * HD, (2 * g + 2) * HD

        def head(i, carry):
            n = g * (NH // KVH) + i
            q = query[n]
            cached = jnp.where(seen, contract(q, store[:, k0:v0]) * HD**-0.5, -jnp.inf)
            fresh = jnp.where(causal, contract(q, kv[:, k0:v0]) * HD**-0.5, -jnp.inf)
            past = contract(q, other[:, k0:v0]) * HD**-0.5
            past = jnp.where(y_hi == 1, past, -jnp.inf)
            top = jnp.maximum(
                jnp.maximum(jnp.max(cached, axis=-1, keepdims=True), jnp.max(past, axis=-1, keepdims=True)),
                jnp.max(fresh, axis=-1, keepdims=True),
            )
            cached, fresh, past = jnp.exp(cached - top), jnp.exp(fresh - top), jnp.exp(past - top)
            total = (
                jnp.sum(cached, axis=-1, keepdims=True)
                + jnp.sum(fresh, axis=-1, keepdims=True)
                + jnp.sum(past, axis=-1, keepdims=True)
            )
            scale = 1.0 / total
            result = dot((cached * scale).astype(BF16), store[:, v0:end])
            result += dot((fresh * scale).astype(BF16), kv[:, v0:end])
            result += dot((past * scale).astype(BF16), other[:, v0:end])
            attended[:, pl.ds(pl.multiple_of(n * HD, HD), HD)] = result.astype(BF16)
            return carry

        lax.fori_loop(0, NH // KVH, head, 0)

    def column(i, square):
        part = dot(attended[...], full[:, pl.ds(pl.multiple_of(i * HD, HD), HD)])
        projected[:, pl.ds(pl.multiple_of(i * HD, HD), HD)] = part
        return square + jnp.sum(part * part, axis=-1, keepdims=True)

    square = lax.fori_loop(0, D // HD, column, jnp.zeros((ROWS, 1), F32))
    scale = lax.rsqrt(square / D + EPS)
    attn = projected[...] * scale * p_gain[...]
    mixed[...] = ((attn + side[...]) / math.sqrt(2.0)).astype(BF16)


def vmem_call(kernel, out_shape, scratch, n_smem, name, args):
    smem = pl.BlockSpec(memory_space=pltpu.SMEM)
    vmem = pl.BlockSpec(memory_space=pltpu.VMEM)
    return pl.pallas_call(
        kernel,
        out_shape=out_shape,
        in_specs=[smem] * n_smem + [vmem] * (len(args) - n_smem),
        out_specs=jax.tree.map(lambda _: vmem, out_shape),
        scratch_shapes=scratch,
        compiler_params=params(),
        name=name,
    )(*args)


def shards(
    tokens, input_gain, w_query, w_keyval, query_gain, key_gain, w_output, laurel_left,
    laurel_right, laurel_gain, post_gain, cache_pool, page_table, cached_len, slot_of,
):
    group, _, _, _, z, y_hi = place()
    own, chip, cross = gather_pages(page_table, slot_of, cache_pool)
    full, chip_in, cross_in = exchange(w_output, chip, cross)
    slot = group * REQ_DEV + z
    start = jnp.sum(jnp.where(slot_of == slot, cached_len, 0))
    position = start + y_hi * ROWS + jnp.arange(ROWS, dtype=jnp.int32)
    inverse = jnp.power(jnp.float32(1000000.0), -jnp.arange(HALF, dtype=F32) * (2.0 / HD))
    angle = position.astype(F32)[:, None] * inverse[None, :]
    query, kv, side = vmem_call(
        project_kernel,
        (
            jax.ShapeDtypeStruct((NH, ROWS, HD), BF16),
            jax.ShapeDtypeStruct((ROWS, KVW), BF16),
            jax.ShapeDtypeStruct((ROWS, D), F32),
        ),
        [pltpu.VMEM((ROWS, D), BF16)],
        0,
        "project",
        (
            tokens, input_gain[None], w_query, w_keyval, query_gain[None], key_gain[None],
            laurel_left, laurel_right, laurel_gain[None], jnp.cos(angle), jnp.sin(angle),
        ),
    )
    other = lax.ppermute(kv, "head", [(2 * i, 2 * i + 1) for i in range(4)])
    return vmem_call(
        attend_kernel,
        jax.ShapeDtypeStruct((ROWS, D), BF16),
        [
            pltpu.VMEM((LMAX, KVW), BF16),
            pltpu.VMEM((ROWS, D), BF16),
            pltpu.VMEM((ROWS, D), F32),
            pltpu.SemaphoreType.DMA((1,)),
        ],
        2,
        "attend",
        (
            cached_len, slot_of, query, kv, other, own, chip_in, cross_in, full, side,
            post_gain[None],
        ),
    )


def solution(mesh):
    in_specs = (
        P(("req", "head"), None),
        P(), P(), P(), P(), P(),
        P("req", None),
        P(), P(), P(), P(),
        P("req", None, None),
        P(), P(), P(),
    )
    out_specs = P(("req", "head"), None)
    return jax.shard_map(shards, mesh=mesh, in_specs=in_specs, out_specs=out_specs, check_vma=False)
```

```python
import math

import jax
import jax.numpy as jnp
import numpy as np
from jax import lax
from jax.experimental import pallas as pl
from jax.experimental.pallas import tpu as pltpu
from jax.sharding import PartitionSpec as P

MESH = pl.DeviceIdType.MESH
F32 = jnp.float32
BF16 = jnp.bfloat16

D = 2048
NH = 8
KVH = 2
PER_KV = NH // KVH
HD = 256
HALF = HD // 2
RANK = 64
REQ_DEV = 4
CH = 512
LMAX = 1024
PAGE = 64
MAXP = 16
POOL = 64
GROUPS = 16
NREQ = 64
ROWS = 256
KVW = 2 * KVH * HD
WROWS = D // GROUPS
UNIT = WROWS // 4
QPAGES = MAXP // 4
HPAGES = QPAGES // 2
EPS = 1e-06
CROSS_AT = MAXP
N_COPIES = 72
VMEM_LIMIT = 64 * 1024 * 1024 - 128 * 1024
INVERSE = np.power(1000000.0, -np.arange(HALF) * (2.0 / HD)).astype(np.float32)[None]


def rms(values):
    return lax.rsqrt(jnp.mean(values * values, axis=-1, keepdims=True) + EPS)


def dot(a, b):
    return jnp.dot(a, b, preferred_element_type=F32)


def contract(a, b):
    return lax.dot_general(a, b, (((1,), (1,)), ((), ())), preferred_element_type=F32)


def rotated(values, cosine, sine):
    a, b = values[:, :HALF], values[:, HALF:]
    return jnp.concatenate([a * cosine - b * sine, b * cosine + a * sine], axis=-1)


def block_kernel(
    table, lens, slots,
    in_gain, q_gain, k_gain, left_t, right, l_gain, p_gain, inverse,
    tokens_hbm, wq_hbm, wkv_hbm, w_ref, pool,
    mixed,
    tokens, wq, wkv, full, store, moved, chip_out, cross_out, cache,
    normed, cosine, sine, query, kv, other, side, attended, projected, tops, totals, sums,
    ssem, rsem, lsem,
):
    group = lax.axis_index("req")
    member = lax.axis_index("head")
    x, yl, c = group // 4, (group // 2) % 2, group % 2
    z, h = member // 2, member % 2

    def dev(ax, ayl, ac, az, ah):
        return (ax * 4 + ayl * 2 + ac, az * 2 + ah)

    xp, xm, x2 = (x + 1) % 4, (x + 3) % 4, (x + 2) % 4
    zp, zm = (z + 1) % 4, (z + 3) % 4
    ol = 1 - yl
    to_xp, to_xm = dev(xp, yl, c, z, h), dev(xm, yl, c, z, h)
    to_zp, to_zm = dev(x, yl, c, zp, h), dev(x, yl, c, zm, h)
    to_s, to_c = dev(x, ol, c, z, h), dev(x, ol, c, z, 1 - h)
    to_p = dev(x, yl, 1 - c, z, h)
    to_o = dev(x, yl, c, z, 1 - h)
    partner = group + 1 - 2 * c
    across = (group + 2 * c - 1 + GROUPS) % GROUPS
    to_t = [(across, z * 2 + h), (across, z * 2 + 1 - h)]

    barrier = pltpu.get_barrier_semaphore()
    peers = [to_xp, to_xm, to_zp, to_zm, to_s, to_c, to_p, to_o] + to_t
    for peer in peers:
        pl.semaphore_signal(barrier, inc=1, device_id=peer, device_id_type=MESH)

    loads = []

    def load(src, dst):
        copy = pltpu.make_async_copy(src, dst, lsem.at[len(loads)])
        copy.start()
        loads.append(copy)
        return copy

    pool_in = load(pool, store)
    tokens_in = load(tokens_hbm, tokens)
    wkv_in = load(wkv_hbm, wkv)
    wq_in = [load(wq_hbm.at[:, pl.ds(i * 2 * HD, 2 * HD)], wq.at[:, pl.ds(i * 2 * HD, 2 * HD)]) for i in range(4)]

    def rows(ax, ayl, unit, n):
        start = (ax * 4 + ayl * 2 + c) * WROWS + unit * UNIT
        return full.at[pl.ds(pl.multiple_of(start, UNIT), n * UNIT)]

    own_in = load(w_ref, rows(x, yl, 0, 4))
    pl.semaphore_wait(barrier, len(peers))

    sent = []
    waited = []

    def copy_of(src, dst, to):
        i = len(sent)
        copy = pltpu.make_async_remote_copy(
            src_ref=src,
            dst_ref=dst,
            send_sem=ssem.at[i],
            recv_sem=rsem.at[i],
            device_id=to,
            device_id_type=MESH,
        )
        sent.append(copy)
        return copy

    def send(src, dst, to):
        copy = copy_of(src, dst, to)
        copy.start()
        return copy

    def landed(*copies):
        for copy in copies:
            if not any(copy is done for done in waited):
                waited.append(copy)
                copy.wait_recv()

    def mine(unit, n):
        return w_ref.at[pl.ds(unit * UNIT, n * UNIT)]

    def pages(az, rel, p):
        half = h if rel == 0 else 1 - h
        return moved.at[pl.ds(CROSS_AT + az * QPAGES + half * HPAGES + p, 1)]

    def relay(ref, to):
        return send(ref, ref, to)

    a1 = [send(mine(0, 2), rows(x, yl, 0, 2), to) for to in (to_xp, to_xm)]
    b1 = [send(mine(2, 1), rows(x, yl, 2, 1), to_s), send(mine(3, 1), rows(x, yl, 3, 1), to_c)]

    slot = group * REQ_DEV + z
    request = lax.fori_loop(
        0, NREQ, lambda i, found: jnp.where(slots[i] == slot, i, found), jnp.int32(0)
    )
    length = lens[request]
    base = group * REQ_DEV
    to_chip, to_cross = base, base
    for i in range(REQ_DEV):
        aim = slots[base + i] // REQ_DEV
        to_chip = jnp.where(aim == partner, base + i, to_chip)
        to_cross = jnp.where(aim == across, base + i, to_cross)

    pool_in.wait()
    first = z * QPAGES + h * HPAGES
    for p in range(HPAGES):
        cross_out[p] = store[table[to_cross, first + p]]

    def pick(p, carry):
        chip_out[p] = store[table[to_chip, p]]
        return carry

    lax.fori_loop(0, MAXP, pick, 0)

    tokens_in.wait()
    inputs = tokens[...].astype(F32)
    normed[...] = (inputs * rms(inputs) * in_gain[...]).astype(BF16)

    crossing = [
        send(cross_out.at[pl.ds(p, 1)], moved.at[pl.ds(CROSS_AT + first + p, 1)], to_t[rel])
        for p in range(HPAGES)
        for rel in range(2)
    ]
    b2 = [send(mine(2, 2), rows(x, yl, 2, 2), to) for to in (to_xp, to_xm)]
    a3 = [[send(mine(0, 1), rows(x, yl, 0, 1), to_s), send(mine(1, 1), rows(x, yl, 1, 1), to_c)]]
    chip_copy = send(chip_out, moved.at[pl.ds(0, MAXP)], to_p)
    rest = [send(w_ref, rows(x, yl, 0, 4), to_p)]

    position = (length + h * ROWS + lax.broadcasted_iota(jnp.int32, (ROWS, 1), 0)).astype(F32)
    angle = position * inverse[...]
    cosine[...] = jnp.cos(angle)
    sine[...] = jnp.sin(angle)

    wkv_in.wait()
    for g in range(KVH):
        k0, v0, end = 2 * g * HD, (2 * g + 1) * HD, (2 * g + 2) * HD
        key = dot(normed[...], wkv[:, k0:v0])
        key = rotated(key * rms(key) * k_gain[...], cosine[...], sine[...])
        kv[:, k0:v0] = key.astype(BF16)
        value = dot(normed[...], wkv[:, v0:end])
        kv[:, v0:end] = (value * rms(value)).astype(BF16)

    landed(*a1)
    a2 = [relay(rows(xm, yl, 0, 1), to_xp), relay(rows(xp, yl, 1, 1), to_xm)]
    for ax in (xm, xp):
        a3.append([relay(rows(ax, yl, 0, 1), to_s), relay(rows(ax, yl, 1, 1), to_c)])
        rest.append(relay(rows(ax, yl, 0, 2), to_p))

    kv_copy = copy_of(kv, other, to_o)

    @pl.when(h == 0)
    def _():
        kv_copy.start()
        other[...] = jnp.zeros_like(other)

    landed(*b1)
    b2y = [relay(rows(x, ol, 2, 2), to) for to in (to_xp, to_xm)]
    rest.append(relay(rows(x, ol, 2, 2), to_p))

    def heads(i):
        wq_in[i].wait()

        def head(j, carry):
            n = 2 * i + j
            raw = dot(normed[...], wq[:, pl.ds(pl.multiple_of(n * HD, HD), HD)])
            raw = rotated(raw * rms(raw) * q_gain[...], cosine[...], sine[...])
            query[n] = raw.astype(BF16) * BF16(HD**-0.5)
            return carry

        lax.fori_loop(0, 2, head, 0)

    ring = []
    ends = [chip_copy]

    def ring_step(p):
        for rel in range(2):
            landed(crossing[2 * p + rel])
            for to in (to_zp, to_zm):
                ring.append(relay(pages(z, rel, p), to))

    def ring_next(p):
        for rel in range(2):
            landed(ring[4 * p + 2 * rel], ring[4 * p + 2 * rel + 1])
            ends.append(relay(pages(zm, 0, p), to_zp) if rel == 0 else relay(pages(zp, 1, p), to_zm))

    heads(0)
    ring_step(0)
    heads(1)
    ring_step(1)
    heads(2)
    landed(*b2)
    b3 = [relay(rows(xm, yl, 2, 1), to_xp), relay(rows(xp, yl, 3, 1), to_xm)]
    for ax in (xm, xp):
        rest.append(relay(rows(ax, yl, 2, 2), to_p))
    heads(3)
    ring_next(0)

    low = contract(normed[...], left_t[...]).astype(BF16)
    u = dot(low, right[...])
    laurel = normed[...].astype(F32) + u * rms(u) * l_gain[...]
    side[...] = tokens[...].astype(F32) + laurel
    ring_next(1)

    causal = lax.broadcasted_iota(jnp.int32, (ROWS, ROWS), 1) <= lax.broadcasted_iota(
        jnp.int32, (ROWS, ROWS), 0
    )

    def fresh_heads(g):
        k0, v0, end = 2 * g * HD, (2 * g + 1) * HD, (2 * g + 2) * HD

        def head(i, carry):
            n = g * PER_KV + i
            q = query[n]
            now = jnp.where(causal, contract(q, kv[:, k0:v0]), -jnp.inf)
            past = jnp.where(h == 1, contract(q, other[:, k0:v0]), -jnp.inf)
            top = jnp.maximum(jnp.max(now, axis=-1, keepdims=True), jnp.max(past, axis=-1, keepdims=True))
            now, past = jnp.exp(now - top), jnp.exp(past - top)
            tops[n] = top
            totals[n] = jnp.sum(now, axis=-1, keepdims=True) + jnp.sum(past, axis=-1, keepdims=True)
            sums[n] = dot(now.astype(BF16), kv[:, v0:end]) + dot(past.astype(BF16), other[:, v0:end])
            return carry

        lax.fori_loop(0, PER_KV, head, 0)

    @pl.when(h == 1)
    def _():
        kv_copy.wait_recv()

    waited.append(kv_copy)
    fresh_heads(0)
    landed(*a2)
    a3.append([relay(rows(x2, yl, 0, 1), to_s), relay(rows(x2, yl, 1, 1), to_c)])
    rest.append(relay(rows(x2, yl, 0, 2), to_p))
    landed(*b2y)
    b3 += [relay(rows(xm, ol, 2, 1), to_xp), relay(rows(xp, ol, 3, 1), to_xm)]
    for ax in (xm, xp):
        rest.append(relay(rows(ax, ol, 2, 2), to_p))
    fresh_heads(1)

    for ax, pair in zip((x, xm, xp), a3[:3]):
        landed(*pair)
        rest.append(relay(rows(ax, ol, 0, 2), to_p))
    landed(*ends)
    home = request // REQ_DEV
    local = home == group
    shift = jnp.where(home == partner, 0, CROSS_AT)

    def settle(p, carry):
        cache[pl.ds(pl.multiple_of(p * PAGE, PAGE), PAGE)] = jnp.where(
            local, store[table[request, p]], moved[shift + p]
        )
        return carry

    lax.fori_loop(0, MAXP, settle, 0)
    seen = lax.broadcasted_iota(jnp.int32, (1, LMAX), 1) < length

    def cached_heads(g):
        k0, v0, end = 2 * g * HD, (2 * g + 1) * HD, (2 * g + 2) * HD

        def head(i, carry):
            n = g * PER_KV + i
            scores = jnp.where(seen, contract(query[n], cache[:, k0:v0]), -jnp.inf)
            top = jnp.maximum(tops[n], jnp.max(scores, axis=-1, keepdims=True))
            keep = jnp.exp(tops[n] - top)
            scores = jnp.exp(scores - top)
            total = totals[n] * keep + jnp.sum(scores, axis=-1, keepdims=True)
            result = sums[n] * keep + dot(scores.astype(BF16), cache[:, v0:end])
            attended[:, pl.ds(pl.multiple_of(n * HD, HD), HD)] = (result / total).astype(BF16)
            return carry

        lax.fori_loop(0, PER_KV, head, 0)

    cached_heads(0)
    landed(*b3)
    rest.append(relay(rows(x2, yl, 2, 2), to_p))
    rest.append(relay(rows(x2, ol, 2, 2), to_p))
    landed(*a3[3])
    rest.append(relay(rows(x2, ol, 0, 2), to_p))
    cached_heads(1)
    for copy in loads[-1:]:
        copy.wait()
    landed(*rest)

    def column(i, square):
        part = dot(attended[...], full[:, pl.ds(pl.multiple_of(i * HD, HD), HD)])
        projected[:, pl.ds(pl.multiple_of(i * HD, HD), HD)] = part
        return square + jnp.sum(part * part, axis=-1, keepdims=True)

    square = lax.fori_loop(0, D // HD, column, jnp.zeros((ROWS, 1), F32))
    scale = lax.rsqrt(square / D + EPS)
    attn = projected[...] * scale * p_gain[...]
    mixed[...] = ((attn + side[...]) / math.sqrt(2.0)).astype(BF16)
    landed(*sent)
    for copy in sent:
        if copy is not kv_copy:
            copy.wait_send()

    @pl.when(h == 0)
    def _():
        kv_copy.wait_send()


def shards(
    tokens, input_gain, w_query, w_keyval, query_gain, key_gain, w_output, laurel_left,
    laurel_right, laurel_gain, post_gain, cache_pool, page_table, cached_len, slot_of,
):
    smem = pl.BlockSpec(memory_space=pltpu.SMEM)
    vmem = pl.BlockSpec(memory_space=pltpu.VMEM)
    stay = pl.BlockSpec(memory_space=pl.ANY)
    return pl.pallas_call(
        block_kernel,
        out_shape=jax.ShapeDtypeStruct((ROWS, D), BF16),
        in_specs=[smem] * 3 + [vmem] * 8 + [stay] * 5,
        out_specs=vmem,
        scratch_shapes=[
            pltpu.VMEM((ROWS, D), BF16),
            pltpu.VMEM((D, NH * HD), BF16),
            pltpu.VMEM((D, KVW), BF16),
            pltpu.VMEM((D, D), BF16),
            pltpu.VMEM((POOL, PAGE, KVW), BF16),
            pltpu.VMEM((2 * MAXP, PAGE, KVW), BF16),
            pltpu.VMEM((MAXP, PAGE, KVW), BF16),
            pltpu.VMEM((HPAGES, PAGE, KVW), BF16),
            pltpu.VMEM((LMAX, KVW), BF16),
            pltpu.VMEM((ROWS, D), BF16),
            pltpu.VMEM((ROWS, HALF), F32),
            pltpu.VMEM((ROWS, HALF), F32),
            pltpu.VMEM((NH, ROWS, HD), BF16),
            pltpu.VMEM((ROWS, KVW), BF16),
            pltpu.VMEM((ROWS, KVW), BF16),
            pltpu.VMEM((ROWS, D), F32),
            pltpu.VMEM((ROWS, D), BF16),
            pltpu.VMEM((ROWS, D), F32),
            pltpu.VMEM((NH, ROWS, 1), F32),
            pltpu.VMEM((NH, ROWS, 1), F32),
            pltpu.VMEM((NH, ROWS, HD), F32),
            pltpu.SemaphoreType.DMA((N_COPIES,)),
            pltpu.SemaphoreType.DMA((N_COPIES,)),
            pltpu.SemaphoreType.DMA((16,)),
        ],
        compiler_params=pltpu.CompilerParams(
            collective_id=0, has_side_effects=True, vmem_limit_bytes=VMEM_LIMIT
        ),
        name="block",
    )(
        page_table, cached_len, slot_of,
        input_gain[None], query_gain[None], key_gain[None], laurel_left.T, laurel_right,
        laurel_gain[None], post_gain[None], jnp.asarray(INVERSE),
        tokens, w_query, w_keyval, w_output, cache_pool,
    )


def solution(mesh):
    in_specs = (
        P(("req", "head"), None),
        P(), P(), P(), P(), P(),
        P("req", None),
        P(), P(), P(), P(),
        P("req", None, None),
        P(), P(), P(),
    )
    out_specs = P(("req", "head"), None)
    return jax.shard_map(shards, mesh=mesh, in_specs=in_specs, out_specs=out_specs, check_vma=False)
```
